32 devices in a mesh: seq: 4 (over y, x), span: 4 (over z), kvg: 2 (over core).
Axes of the slice: x: 2, y: 2, z: 4, core: 2. Of those that a mesh axis runs over, the one named last changes fastest.
Arguments:
- query_rows: bfloat16 [8704, 1792], P(('seq', 'span'), 'kvg'), parts along dimension 0, may hold values from -256 to 256
- key_rows: bfloat16 [8704, 256], P(('seq', 'span'), 'kvg'), parts along dimension 0, may hold values from -6 to 6
- value_rows: bfloat16 [8704, 256], P(('seq', 'span'), 'kvg'), parts along dimension 0, may hold values from -6 to 6
- out_grad: bfloat16 [8704, 1792], P(('seq', 'span'), 'kvg'), parts along dimension 0, may hold values from -6 to 6
- ratios: int32 [16], P('seq'), parts along dimension 0, may hold values from 16 to 64, as said below
Outputs:
- attended: bfloat16 [8704, 1792], P(('seq', 'span'), 'kvg'), parts along dimension 0
- query_grad: bfloat16 [8704, 1792], P(('seq', 'span'), 'kvg'), parts along dimension 0
- key_grad: bfloat16 [8704, 256], P(('seq', 'span'), 'kvg'), parts along dimension 0
- value_grad: bfloat16 [8704, 256], P(('seq', 'span'), 'kvg'), parts along dimension 0
The draws below stay inside these ranges and needn't reach their ends.
There are 4 independent parts, one for each index of `seq`. The reference program is written for one: setup_inputs(seed, part) draws one part's arguments, and reference() takes and returns one part's arrays. A program takes and returns all parts, laid end to end along the dimension named above; each array names one. Nothing has to cross between parts.
Inputs may be any that keep to these rules, and one draw needn't show every extreme that they name: `ratios`: every ratio is 16, 32 or 64, and some span of every sequence has 16.
All inputs are finite; a program needn't handle non-finite values.
Results may differ from the reference program's by a relative error of at most 0.0096.
Values may be sent and summed in bfloat16 or wider, within the bound.
A program may use at most 64 MiB of HBM per device.

```python
import jax
import jax.numpy as jnp
from jax import lax

SPAN = 512
RMIN = 16
HD = 128
QPG = 7
GROUPS = 2
BMAX = 32
SEG = 544
NCH = 4
ROWS = 2176
NB = 128


def pair_draw(key):
    base_query = 2.0 * jax.random.normal(jax.random.fold_in(key, 101), (ROWS, GROUPS * QPG * HD), jnp.float32)
    query_draw = jnp.clip(base_query, -12.0, 12.0)
    key_draw = jnp.clip(jax.random.normal(jax.random.fold_in(key, 202), (ROWS, GROUPS * HD), jnp.float32), -6.0, 6.0)
    return (query_draw, key_draw)


def draw_query_rows(key, part):
    return pair_draw(key)[0].astype(jnp.bfloat16)


def draw_key_rows(key, part):
    return pair_draw(key)[1].astype(jnp.bfloat16)


def draw_ratios(key, part):
    powers = jax.random.randint(jax.random.fold_in(key, 404), (NCH,), 0, 3, dtype=jnp.int32)
    chosen = jax.random.randint(jax.random.fold_in(key, 505), (), 0, NCH, dtype=jnp.int32)
    powers = jnp.where(jnp.arange(NCH, dtype=jnp.int32) == chosen, 0, powers)
    return jnp.where(powers == 0, RMIN, jnp.where(powers == 1, 2 * RMIN, 4 * RMIN)).astype(jnp.int32)


def steps_of(rng, dims, cuts, least, top_value):
    gain, own = 1.0, jax.random.fold_in(rng, 6)
    for dim, shards_of in cuts:
        steps = jnp.exp(jax.random.uniform(jax.random.fold_in(own, dim), (shards_of,), jnp.float32, least / len(cuts), top_value / len(cuts)))
        gain = gain * jnp.repeat(steps, dims[dim] // shards_of).reshape([-1 if axis == dim else 1 for axis in range(len(dims))])
    return gain


def gaussian(key, extent, deviation, limit, split=(), held_as=jnp.bfloat16):
    values = deviation * jax.random.normal(key, extent, jnp.float32)
    if split:
        values = values * steps_of(key, extent, split, -0.22, 0.18)
    return jnp.clip(values, -limit, limit).astype(held_as)


def setup_inputs(seed: int = 0, part: int = 0) -> dict:
    streams_of = jax.random.split(jax.random.key(seed), 6)
    part_splits = jax.random.split(jax.random.fold_in(streams_of[5], part), 6)
    query_rows = draw_query_rows(jax.random.fold_in(jax.random.fold_in(streams_of[5], part), 71), part)
    key_rows = draw_key_rows(jax.random.fold_in(jax.random.fold_in(streams_of[5], part), 71), part)
    value_rows = gaussian(part_splits[2], (ROWS, GROUPS * HD), 1.0, 6.0, ((0, 4), (1, 2)))
    out_grad = gaussian(part_splits[3], (ROWS, GROUPS * QPG * HD), 1.0, 6.0, ((0, 4), (1, 2)))
    ratios = draw_ratios(jax.random.fold_in(jax.random.fold_in(streams_of[5], part), 71), part)
    return {"query_rows": query_rows, "key_rows": key_rows, "value_rows": value_rows, "out_grad": out_grad, "ratios": ratios}


floor_score = -1.0e30


def product(pattern, first_arg, second_arg):
    return jnp.einsum(pattern, first_arg.astype(jnp.float32), second_arg.astype(jnp.float32))


def build_masks(ratios, first_span, local_spans):
    counts = SPAN // ratios
    slot_ids = jnp.arange(BMAX, dtype=jnp.int32)
    live_slots = (slot_ids[None, :] < counts[:, None]).reshape(-1)
    span_ids = first_span + jnp.arange(local_spans, dtype=jnp.int32)
    owner_span = jnp.arange(live_slots.shape[0], dtype=jnp.int32) // BMAX
    beacon_mask = (owner_span[None, :] < span_ids[:, None]) & live_slots[None, :]
    local_ratio = lax.dynamic_slice_in_dim(ratios, first_span, local_spans)
    local_count = SPAN // local_ratio
    positions = jnp.arange(SEG, dtype=jnp.int32)
    is_beacon = positions >= SPAN
    slot_of = positions - SPAN
    key_order = jnp.where(is_beacon[None, :], (slot_of[None, :] + 1) * local_ratio[:, None] - 1, positions[None, :])
    live_row = jnp.logical_not(is_beacon[None, :]) | (slot_of[None, :] < local_count[:, None])
    raw_key = jnp.logical_not(is_beacon)[None, None, :] & (key_order[:, None, :] <= key_order[:, :, None])
    beacon_key = is_beacon[None, :, None] & is_beacon[None, None, :] & live_row[:, None, :] & (positions[None, None, :] <= positions[None, :, None])
    return beacon_mask, raw_key | beacon_key, live_row.astype(jnp.float32)


def attend_head(query_head, grad_head, beacon_keys, beacon_values, own_keys, own_values, beacon_mask, own_mask, live_rows):
    score_scale = HD ** -0.5
    beacon_scores = jnp.where(beacon_mask[:, None, :], product("csd,bd->csb", query_head, beacon_keys) * score_scale, floor_score)
    own_scores = jnp.where(own_mask, product("csd,ctd->cst", query_head, own_keys) * score_scale, floor_score)
    row_top = jnp.maximum(jnp.max(beacon_scores, -1), jnp.max(own_scores, -1))
    row_total = jnp.sum(jnp.exp(beacon_scores - row_top[..., None]), -1) + jnp.sum(jnp.exp(own_scores - row_top[..., None]), -1)
    row_lse = row_top + jnp.log(row_total)
    beacon_probs = jnp.exp(beacon_scores - row_lse[..., None])
    own_probs = jnp.exp(own_scores - row_lse[..., None])
    beacon_weights = beacon_probs.astype(jnp.bfloat16)
    own_weights = own_probs.astype(jnp.bfloat16)
    mixed_rows = product("csb,bd->csd", beacon_weights, beacon_values) + product("cst,ctd->csd", own_weights, own_values)
    attended = (mixed_rows * live_rows[..., None]).astype(jnp.bfloat16)
    grad_rows = grad_head * live_rows.astype(jnp.bfloat16)[..., None]
    row_delta = jnp.sum(grad_rows.astype(jnp.float32) * attended.astype(jnp.float32), -1)
    beacon_sgrad = (beacon_probs * (product("csd,bd->csb", grad_rows, beacon_values) - row_delta[..., None])).astype(jnp.bfloat16)
    own_sgrad = (own_probs * (product("csd,ctd->cst", grad_rows, own_values) - row_delta[..., None])).astype(jnp.bfloat16)
    query_grad = (score_scale * (product("csb,bd->csd", beacon_sgrad, beacon_keys) + product("cst,ctd->csd", own_sgrad, own_keys))).astype(jnp.bfloat16)
    beacon_kgrad = score_scale * product("csb,csd->bd", beacon_sgrad, query_head)
    beacon_vgrad = product("csb,csd->bd", beacon_weights, grad_rows)
    own_kgrad = score_scale * product("cst,csd->ctd", own_sgrad, query_head)
    own_vgrad = product("cst,csd->ctd", own_weights, grad_rows)
    return attended, query_grad, beacon_kgrad, beacon_vgrad, own_kgrad, own_vgrad


def reference(query_rows, key_rows, value_rows, out_grad, ratios):
    beacon_mask, own_mask, live_rows = build_masks(ratios, 0, NCH)
    query_blocks = query_rows.reshape(NCH, SEG, GROUPS, QPG, HD)
    grad_blocks = out_grad.reshape(NCH, SEG, GROUPS, QPG, HD)
    key_blocks = key_rows.reshape(NCH, SEG, GROUPS, HD)
    value_blocks = value_rows.reshape(NCH, SEG, GROUPS, HD)
    attended_parts, query_parts, key_parts, value_parts = [], [], [], []
    for group_index in range(GROUPS):
        own_keys = key_blocks[:, :, group_index]
        own_values = value_blocks[:, :, group_index]
        beacon_keys = own_keys[:, SPAN:].reshape(NB, HD)
        beacon_values = own_values[:, SPAN:].reshape(NB, HD)
        beacon_ksum = jnp.zeros((NB, HD), jnp.float32)
        beacon_vsum = jnp.zeros((NB, HD), jnp.float32)
        own_ksum = jnp.zeros((NCH, SEG, HD), jnp.float32)
        own_vsum = jnp.zeros((NCH, SEG, HD), jnp.float32)
        head_outputs, head_grads = [], []
        for head_index in range(QPG):
            result = attend_head(query_blocks[:, :, group_index, head_index], grad_blocks[:, :, group_index, head_index], beacon_keys, beacon_values, own_keys, own_values, beacon_mask, own_mask, live_rows)
            head_outputs.append(result[0])
            head_grads.append(result[1])
            beacon_ksum = beacon_ksum + result[2]
            beacon_vsum = beacon_vsum + result[3]
            own_ksum = own_ksum + result[4]
            own_vsum = own_vsum + result[5]
        attended_parts.append(jnp.stack(head_outputs, 2))
        query_parts.append(jnp.stack(head_grads, 2))
        key_total = jnp.concatenate([own_ksum[:, :SPAN], own_ksum[:, SPAN:] + beacon_ksum.reshape(NCH, BMAX, HD)], 1)
        value_total = jnp.concatenate([own_vsum[:, :SPAN], own_vsum[:, SPAN:] + beacon_vsum.reshape(NCH, BMAX, HD)], 1)
        key_parts.append(key_total.astype(jnp.bfloat16))
        value_parts.append(value_total.astype(jnp.bfloat16))
    attended = jnp.stack(attended_parts, 2).reshape(ROWS, GROUPS * QPG * HD)
    query_grad = jnp.stack(query_parts, 2).reshape(ROWS, GROUPS * QPG * HD)
    key_grad = jnp.stack(key_parts, 2).reshape(ROWS, GROUPS * HD)
    value_grad = jnp.stack(value_parts, 2).reshape(ROWS, GROUPS * HD)
    return attended, query_grad, key_grad, value_grad
```

```python
import functools
import math

import jax
import jax.numpy as jnp
from jax import lax
from jax.experimental import pallas as pl
from jax.experimental.pallas import tpu as pltpu
from jax.sharding import PartitionSpec as P

SPAN = 512
HD = 128
BMAX = 32
BLK = 256

SCALE = HD ** (-0.5)
SCALE_LOG2E = SCALE * math.log2(math.e)
FLOOR = -1e30

f32 = jnp.float32
bf16 = jnp.bfloat16


def nt(a, b):
    return lax.dot_general(a, b, (((1,), (1,)), ((), ())), preferred_element_type=f32)


def nn(a, b):
    return lax.dot_general(a, b, (((1,), (0,)), ((), ())), preferred_element_type=f32)


def interleave(blocks):
    waiting, active = list(blocks), []
    while waiting or active:
        if waiting:
            active.append(waiting.pop(0))
        active = [block for block in active if next(block, "end") != "end"]


def kernel(
    n, heads,
    ratios_ref, q_hbm, k_hbm, v_hbm, g_hbm,
    o_hbm, dq_hbm, dk_out, dv_out,
    q_s, g_s, k_s, v_s, kt_s, vt_s, kb_s, vb_s, kbt_s, vbt_s,
    e_s, ot_s, stat_s, bias_s, bbias_s, term_s, recv_s, dk_s, dv_s, o_s, dq_s,
    in_sem, q_sem, g_sem, qb_sem, gb_sem, o_sem, dq_sem, ob_sem, dqb_sem,
    kv_send, kv_recv, term_send, term_recv,
):
    me = lax.axis_index("span")
    chunks = SPAN // BLK
    last = heads * chunks
    nb = n * BMAX

    barrier = pltpu.get_barrier_semaphore()
    for step in range(1, n):
        pl.semaphore_signal(
            barrier, inc=1, device_id={"span": lax.rem(me + step, n)},
            device_id_type=pl.DeviceIdType.MESH,
        )

    def head_cols(h):
        return pl.ds(h * HD, HD)

    def head_rows(h):
        return pl.ds(h * SPAN, SPAN)

    def block_rows(b):
        return pl.ds(b * BLK, BLK)

    def q_copy(h):
        return pltpu.make_async_copy(
            q_hbm.at[pl.ds(0, SPAN), head_cols(h)], q_s.at[head_rows(h)], q_sem.at[h]
        )

    def g_copy(h):
        return pltpu.make_async_copy(
            g_hbm.at[pl.ds(0, SPAN), head_cols(h)], g_s.at[head_rows(h)], g_sem.at[h]
        )

    def tail_copy(src, dst, sem, h):
        return pltpu.make_async_copy(
            src.at[pl.ds(SPAN, BMAX), pl.ds(h * HD, HD)],
            dst.at[pl.ds(last * BLK + h * BMAX, BMAX)],
            sem.at[h],
        )

    k_copy = pltpu.make_async_copy(k_hbm.at[pl.ds(0, SPAN)], k_s, in_sem.at[0])
    v_copy = pltpu.make_async_copy(v_hbm.at[pl.ds(0, SPAN)], v_s, in_sem.at[1])
    mine = pl.ds(pl.multiple_of(me * BMAX, BMAX), BMAX)
    kb_copy = pltpu.make_async_copy(
        k_hbm.at[pl.ds(SPAN, BMAX)], kb_s.at[mine], in_sem.at[2]
    )
    vb_copy = pltpu.make_async_copy(
        v_hbm.at[pl.ds(SPAN, BMAX)], vb_s.at[mine], in_sem.at[3]
    )
    k_copy.start()
    v_copy.start()
    q_copy(0).start()
    kb_copy.start()
    vb_copy.start()
    for h in range(1, heads):
        q_copy(h).start()
    for h in range(heads):
        tail_copy(q_hbm, q_s, qb_sem, h).start()
    for h in range(heads):
        g_copy(h).start()
    for h in range(heads):
        tail_copy(g_hbm, g_s, gb_sem, h).start()

    own_ratio = ratios_ref[me]
    key_id = lax.broadcasted_iota(jnp.int32, (nb, BLK), 0)
    lane_slot = lax.rem(lax.broadcasted_iota(jnp.int32, (nb, BLK), 1), BMAX)
    key_slot = lax.rem(key_id, BMAX)
    key_span = key_id // BMAX
    key_ratio = jnp.zeros((nb, BLK), jnp.int32)
    for s in range(n):
        key_ratio = jnp.where(key_span == s, ratios_ref[s], key_ratio)
    live = (key_slot + 1) * key_ratio <= SPAN
    before = live & (key_span < me)
    bias_s[...] = jnp.where(before, 0.0, FLOOR)
    bbias_s[...] = jnp.where(
        before | (live & (key_span == me) & (key_slot <= lane_slot)), 0.0, FLOOR
    )
    term_s[...] = jnp.zeros_like(term_s)
    dk_s[...] = jnp.zeros_like(dk_s)
    dv_s[...] = jnp.zeros_like(dv_s)
    pad = BLK - heads * BMAX
    q_s[pl.ds(last * BLK + heads * BMAX, pad), :] = jnp.zeros((pad, HD), bf16)
    g_s[pl.ds(last * BLK + heads * BMAX, pad), :] = jnp.zeros((pad, HD), bf16)

    pl.semaphore_wait(barrier, n - 1)

    def kv_copies(step):
        peer = lax.rem(me + step, n)
        return [
            pltpu.make_async_remote_copy(
                src_ref=src.at[pl.ds(SPAN, BMAX)], dst_ref=dst.at[mine],
                send_sem=kv_send.at[i, step - 1], recv_sem=kv_recv.at[i, step - 1],
                device_id={"span": peer}, device_id_type=pl.DeviceIdType.MESH,
            )
            for i, (src, dst) in enumerate(((k_hbm, kb_s), (v_hbm, vb_s)))
        ]

    for step in range(1, n):
        for copy in kv_copies(step):
            copy.start()

    k_copy.wait()
    v_copy.wait()
    kt_s[...] = k_s[...].T
    vt_s[...] = v_s[...].T

    row = lax.broadcasted_iota(jnp.int32, (BLK, BLK), 0)
    col = lax.broadcasted_iota(jnp.int32, (BLK, BLK), 1)

    def own_scores(b, masks, wait=None):
        if wait is not None:
            wait()
        query = q_s[block_rows(b), :]
        scores = nt(k_s[pl.ds(0, len(masks) * BLK), :], query)
        scores = [scores[c * BLK : (c + 1) * BLK] for c in range(len(masks))]
        scores = [
            s if mask is None else jnp.where(mask, s, FLOOR)
            for s, mask in zip(scores, masks)
        ]
        yield
        top = functools.reduce(
            jnp.maximum, [jnp.max(s, axis=0, keepdims=True) for s in scores]
        )
        yield
        total = jnp.zeros((1, BLK), f32)
        parts = []
        for c, s in enumerate(scores):
            e = jnp.exp2((s - top) * SCALE_LOG2E)
            total = total + jnp.sum(e, axis=0, keepdims=True)
            parts.append(e.astype(bf16))
            e_s[b, pl.ds(c * BLK, BLK), :] = parts[-1]
        yield
        mixed = nn(vt_s[:, pl.ds(0, len(masks) * BLK)], jnp.concatenate(parts, 0))
        ot_s[b] = mixed
        stat_s[b, 0:1, :] = top
        stat_s[b, 1:2, :] = total

    reach = (lax.rem(col, BMAX) + 1) * own_ratio

    def tails_in(src, dst, sem):
        for h in range(heads):
            tail_copy(src, dst, sem, h).wait()

    interleave(
        [
            own_scores(
                h * chunks + t, [None] * t + [row <= col],
                q_copy(h).wait if t == 0 else None,
            )
            for h in range(heads)
            for t in range(chunks)
        ]
        + [
            own_scores(
                last, [row + c * BLK < reach for c in range(chunks)],
                functools.partial(tails_in, q_hbm, q_s, qb_sem),
            )
        ]
    )

    kb_copy.wait()
    vb_copy.wait()
    for step in range(1, n):
        for copy in kv_copies(step):
            copy.wait()
    kbt_s[...] = kb_s[...].T
    vbt_s[...] = vb_s[...].T
    ones = jnp.ones((8, HD), bf16)

    def beacon_part(b, bias, live_rows, wait=None, done=None):
        if wait is not None:
            wait()
        query = q_s[block_rows(b), :]
        grad = g_s[block_rows(b), :]
        if live_rows is not None:
            grad = jnp.where(live_rows, grad.astype(f32), 0.0).astype(bf16)
            g_s[block_rows(b), :] = grad
        scores = nt(kb_s[...], query) + bias[...]
        yield
        own_top = stat_s[b, 0:1, :]
        top = jnp.maximum(own_top, jnp.max(scores, axis=0, keepdims=True))
        e = jnp.exp2((scores - top) * SCALE_LOG2E)
        shrink = jnp.exp2((own_top - top) * SCALE_LOG2E)
        total = shrink * stat_s[b, 1:2, :] + jnp.sum(e, axis=0, keepdims=True)
        inverse = 1.0 / total
        factor = shrink * inverse
        probs = e * inverse
        weights = probs.astype(bf16)
        yield
        out = (ot_s[b] * factor + nn(vbt_s[...], weights)).T
        if live_rows is not None:
            out = jnp.where(live_rows, out, 0.0)
        out = out.astype(bf16)
        o_s[block_rows(b), :] = out
        if done is not None:
            done()
        yield
        terms = grad.astype(f32) * out.astype(f32)
        high = terms.astype(bf16)
        low = (terms - high.astype(f32)).astype(bf16)
        delta = (nt(ones, high) + nt(ones, low))[0:1, :]
        slope = nt(vb_s[...], grad)
        yield
        sgrad = (probs * (slope - delta)).astype(bf16)
        yield
        term_s[:, 0:HD] += nn(sgrad, query)
        term_s[:, HD : 2 * HD] += nn(weights, grad)
        ot_s[b] = nn(kbt_s[...], sgrad)
        stat_s[b, 0:1, :] = factor
        stat_s[b, 1:2, :] = delta

    def o_copy(h):
        return pltpu.make_async_copy(
            o_s.at[head_rows(h)], o_hbm.at[pl.ds(0, SPAN), head_cols(h)], o_sem.at[h]
        )

    def dq_copy(h):
        return pltpu.make_async_copy(
            dq_s.at[head_rows(h)], dq_hbm.at[pl.ds(0, SPAN), head_cols(h)], dq_sem.at[h]
        )

    def tail_out(src, dst, sem, h):
        return pltpu.make_async_copy(
            src.at[pl.ds(last * BLK + h * BMAX, BMAX)],
            dst.at[pl.ds(SPAN, BMAX), pl.ds(h * HD, HD)],
            sem.at[h],
        )

    def tails_out(src, dst, sem):
        for h in range(heads):
            tail_out(src, dst, sem, h).start()

    row_slot = lax.rem(lax.broadcasted_iota(jnp.int32, (BLK, HD), 0), BMAX)
    interleave(
        [
            beacon_part(
                h * chunks + t, bias_s, None,
                g_copy(h).wait if t == 0 else None,
                o_copy(h).start if t == chunks - 1 else None,
            )
            for h in range(heads)
            for t in range(chunks)
        ]
        + [
            beacon_part(
                last, bbias_s, (row_slot + 1) * own_ratio <= SPAN,
                functools.partial(tails_in, g_hbm, g_s, gb_sem),
                functools.partial(tails_out, o_s, o_hbm, ob_sem),
            )
        ]
    )

    def own_part(b, count, done=None):
        query = q_s[block_rows(b), :]
        grad = g_s[block_rows(b), :]
        factor = stat_s[b, 0:1, :]
        delta = stat_s[b, 1:2, :]
        keys = pl.ds(0, count * BLK)
        slope = nt(v_s[keys, :], grad)
        yield
        probs = e_s[b, keys, :].astype(f32) * factor
        sgrad = (probs * (slope - delta)).astype(bf16)
        yield
        dk_s[keys, :] += nn(sgrad, query)
        dv_s[keys, :] += nn(probs.astype(bf16), grad)
        dqt = ot_s[b] + nn(kt_s[:, keys], sgrad)
        yield
        dq_s[block_rows(b), :] = (dqt * SCALE).T.astype(bf16)
        if done is not None:
            done()

    def term_copy(step):
        peer = lax.rem(me + step, n)
        return pltpu.make_async_remote_copy(
            src_ref=term_s.at[pl.ds(pl.multiple_of(peer * BMAX, BMAX), BMAX)],
            dst_ref=recv_s.at[step - 1],
            send_sem=term_send.at[step - 1], recv_sem=term_recv.at[step - 1],
            device_id={"span": peer}, device_id_type=pl.DeviceIdType.MESH,
        )

    interleave(
        [own_part(last, chunks, functools.partial(tails_out, dq_s, dq_hbm, dqb_sem))]
    )
    for step in range(1, n):
        term_copy(step).start()

    interleave(
        [
            own_part(
                h * chunks + t, t + 1, dq_copy(h).start if t == chunks - 1 else None
            )
            for h in range(heads)
            for t in range(chunks)
        ]
    )

    dk_out[0:SPAN, :] = (dk_s[...] * SCALE).astype(bf16)
    dv_out[0:SPAN, :] = dv_s[...].astype(bf16)
    total = term_s[mine, :]
    for step in range(1, n):
        term_copy(step).wait()
        total = total + recv_s[step - 1]
    dk_out[SPAN : SPAN + BMAX, :] = (total[:, 0:HD] * SCALE).astype(bf16)
    dv_out[SPAN : SPAN + BMAX, :] = total[:, HD : 2 * HD].astype(bf16)

    for h in range(heads):
        o_copy(h).wait()
        dq_copy(h).wait()
        tail_out(o_s, o_hbm, ob_sem, h).wait()
        tail_out(dq_s, dq_hbm, dqb_sem, h).wait()


def local(n, query_rows, key_rows, value_rows, out_grad, ratios):
    heads = query_rows.shape[1] // HD
    chunks = SPAN // BLK
    blocks = heads * chunks + 1
    nb = n * BMAX
    any_spec = pl.BlockSpec(memory_space=pltpu.HBM)
    vmem_spec = pl.BlockSpec(memory_space=pltpu.VMEM)
    dma = pltpu.SemaphoreType.DMA
    return pl.pallas_call(
        functools.partial(kernel, n, heads),
        out_shape=(
            jax.ShapeDtypeStruct(query_rows.shape, bf16),
            jax.ShapeDtypeStruct(query_rows.shape, bf16),
            jax.ShapeDtypeStruct(key_rows.shape, bf16),
            jax.ShapeDtypeStruct(value_rows.shape, bf16),
        ),
        in_specs=[pl.BlockSpec(memory_space=pltpu.SMEM)] + [any_spec] * 4,
        out_specs=(pl.BlockSpec(memory_space=pl.ANY), pl.BlockSpec(memory_space=pl.ANY), vmem_spec, vmem_spec),
        scratch_shapes=[
            pltpu.VMEM((blocks * BLK, HD), bf16),
            pltpu.VMEM((blocks * BLK, HD), bf16),
            pltpu.VMEM((SPAN, HD), bf16),
            pltpu.VMEM((SPAN, HD), bf16),
            pltpu.VMEM((HD, SPAN), bf16),
            pltpu.VMEM((HD, SPAN), bf16),
            pltpu.VMEM((nb, HD), bf16),
            pltpu.VMEM((nb, HD), bf16),
            pltpu.VMEM((HD, nb), bf16),
            pltpu.VMEM((HD, nb), bf16),
            pltpu.VMEM((blocks, SPAN, BLK), bf16),
            pltpu.VMEM((blocks, HD, BLK), f32),
            pltpu.VMEM((blocks, 8, BLK), f32),
            pltpu.VMEM((nb, BLK), f32),
            pltpu.VMEM((nb, BLK), f32),
            pltpu.VMEM((nb, 2 * HD), f32),
            pltpu.VMEM((n - 1, BMAX, 2 * HD), f32),
            pltpu.VMEM((SPAN, HD), f32),
            pltpu.VMEM((SPAN, HD), f32),
            pltpu.VMEM((blocks * BLK, HD), bf16),
            pltpu.VMEM((blocks * BLK, HD), bf16),
            dma((4,)), dma((heads,)), dma((heads,)), dma((heads,)), dma((heads,)),
            dma((heads,)), dma((heads,)), dma((heads,)), dma((heads,)),
            dma((2, n - 1)), dma((2, n - 1)), dma((n - 1,)), dma((n - 1,)),
        ],
        compiler_params=pltpu.CompilerParams(
            collective_id=0, has_side_effects=True, vmem_limit_bytes=67043328
        ),
        name="beacon_attention",
    )(ratios, query_rows, key_rows, value_rows, out_grad)


def solution(mesh):
    rows = P(("seq", "span"), "kvg")
    return jax.shard_map(
        functools.partial(local, mesh.shape["span"]),
        mesh=mesh,
        in_specs=(rows, rows, rows, rows, P("seq")),
        out_specs=(rows, rows, rows, rows),
        check_vma=False,
    )
```
